256 devices in a mesh: dp: 16 (over y, z_lo), mp: 16 (over z_hi, x, core).
Axes of the slice: x: 4, y: 4, z: 8 (z_hi: 2, z_lo: 4; z = z_hi * 4 + z_lo), core: 2. Of those that a mesh axis runs over, the one named last changes fastest.
Arguments:
- frames: float32 [7168, 1536], P('dp', 'mp'), may hold values from -6 to 6
- norm_gain: float32 [1536], replicated, may hold values from 0.1 to 1.9
- w_in: float32 [1536, 6144], P(None, 'mp'), may hold values from -0.15625 to 0.15625
- w_out: float32 [6144, 1536], P('mp'), may hold values from -0.078125 to 0.078125
- head_weight: float32 [16, 1536, 1024], P('mp'), as said below
- teacher: int32 [16, 7168], P('mp', 'dp'), may hold values from 0 to 1023
Outputs:
- loss: float32 [], replicated
- grad_in: float32 [1536, 6144], P('dp', 'mp')
- grad_out: float32 [6144, 1536], P('mp', 'dp')
- grad_head: float32 [16, 1536, 1024], P('mp', 'dp')
The draws below stay inside these ranges and needn't reach their ends.
Inputs may be any that keep to these rules, and one draw needn't show every extreme that they name: `head_weight`: each head's projection has independent entries of order 1536 ** -0.5 times a per-code factor.
All inputs are finite; a program needn't handle non-finite values.
Results may differ from the reference program's by a relative error of at most 0.0003.
Values sent between devices are 32-bit elements; how exact they have to be, the bound alone decides.
No kernel may reach another device: no remote copies, remote signals or barrier semaphores. Data moves between devices by JAX's collectives and lax.ppermute only.
A program may use at most 128 MiB of HBM per device.

```python
import jax
import jax.numpy as jnp
from jax import lax

D = 1536
FF = 6144
CODES = 1024
HEADS = 16
FRAMES = 7168


def draw_head_weight(key, part):
    base_key, scale_key = jax.random.split(jax.random.fold_in(key, 4177), 2)
    values = jax.random.normal(base_key, (HEADS, D, CODES), jnp.float32) * D ** (-0.5)
    factor = jnp.exp(jax.random.uniform(scale_key, (HEADS, 1, CODES), jnp.float32, -0.7, 0.7))
    return values * factor


def touch_ends(array, rng, least, largest):
    longest = array.shape.index(max(array.shape))
    spots = []
    for shift in (0, 1):
        where = [jax.random.randint(jax.random.fold_in(rng, axis), (), 0, length) for axis, length in enumerate(array.shape)]
        where[longest] = (where[longest] + shift) % array.shape[longest]
        spots.append(tuple(where))
    return array.at[spots[0]].set(least).at[spots[1]].set(largest)


def level_of(own_key, dims, pieces, smallest, top_value):
    def one(dim, blocks):
        heights = jax.random.uniform(jax.random.fold_in(jax.random.fold_in(own_key, 6), dim), (blocks,), jnp.float32, smallest / len(pieces), top_value / len(pieces))
        return jnp.repeat(jnp.exp(heights), dims[dim] // blocks).reshape((-1,) + (1,) * (len(dims) - dim - 1))

    factor_of = one(*pieces[0])
    for cut in pieces[1:]:
        factor_of = factor_of * one(*cut)
    return factor_of


def bell_draw(stream_key, dims, width, limit, pieces=(), held_as=jnp.bfloat16):
    factor_of = level_of(stream_key, dims, pieces, -0.22, 0.18) if pieces else 1.0
    values = jax.random.normal(stream_key, dims, jnp.float32) * width * factor_of
    return jnp.minimum(jnp.maximum(values, -limit), limit).astype(held_as)


def setup_inputs(seed: int = 0) -> dict:
    seeds = jax.random.split(jax.random.key(seed), 7)
    return {
        "frames": bell_draw(seeds[0], (FRAMES, D), 1.0, 6.0, ((0, 16), (1, 16)), jnp.float32),
        "norm_gain": jnp.clip(1.0 + 0.18 * jax.random.normal(seeds[1], (D,), jnp.float32), 0.1, 1.9),
        "w_in": bell_draw(seeds[2], (D, FF), D ** -0.5, 0.15625, ((1, 16),), jnp.float32),
        "w_out": bell_draw(seeds[3], (FF, D), FF ** -0.5, 0.078125, ((0, 16),), jnp.float32),
        "head_weight": draw_head_weight(jax.random.fold_in(seeds[6], 71), 0),
        "teacher": touch_ends(jax.random.randint(seeds[5], (HEADS, FRAMES), 0, CODES), jax.random.fold_in(seeds[5], 1), 0, CODES - 1).astype(jnp.int32),
    }


HI = lax.Precision.HIGHEST

def reference(frames, norm_gain, w_in, w_out, head_weight, teacher):
    mean = lax.optimization_barrier(jnp.mean(frames, axis=1, keepdims=True))
    centred = frames - mean
    var = lax.optimization_barrier(jnp.mean(centred * centred, axis=1, keepdims=True))
    normed = centred * lax.rsqrt(var + 1e-05) * norm_gain
    pre = jnp.dot(normed, w_in, precision=HI)
    sig = jax.nn.sigmoid(pre)
    act = pre * sig
    mixed = frames + 0.5 * jnp.dot(act, w_out, precision=HI)
    codes = jnp.arange(head_weight.shape[2], dtype=jnp.int32)

    def one_head(carry, item):
        weight, target = item
        logits = jnp.dot(mixed, weight, precision=HI)
        top = lax.optimization_barrier(jnp.max(logits, axis=1, keepdims=True))
        expo = jnp.exp(logits - top)
        total = lax.optimization_barrier(jnp.sum(expo, axis=1, keepdims=True))
        lse = top + jnp.log(total)
        onehot = (target[:, None] == codes[None, :]).astype(jnp.float32)
        picked = lax.optimization_barrier(jnp.sum(logits * onehot, axis=1, keepdims=True))
        dlogits = expo / total - onehot
        grad = jnp.dot(mixed.T, dlogits, precision=HI)
        loss_acc, dmix = carry
        dmix = dmix + jnp.dot(dlogits, weight.T, precision=HI)
        loss_acc = loss_acc + jnp.sum(lse - picked)
        return ((loss_acc, dmix), grad)
    start = (jnp.zeros((), jnp.float32), jnp.zeros_like(mixed))
    (loss_total, dmixed), grad_head = lax.scan(one_head, start, (head_weight, teacher))
    dffn = 0.5 * dmixed
    grad_out = jnp.dot(act.T, dffn, precision=HI)
    dact = jnp.dot(dffn, w_out.T, precision=HI)
    dpre = dact * sig * (1.0 + pre * (1.0 - sig))
    grad_in = jnp.dot(normed.T, dpre, precision=HI)
    loss = loss_total / (FRAMES * HEADS)
    return (loss, grad_in, grad_out, grad_head)
```

```python
import jax
import jax.numpy as jnp
from jax import lax
from jax.sharding import PartitionSpec as P

F32 = jnp.float32
BF16 = jnp.bfloat16


def mp_perm(f):
    out = []
    for i in range(16):
        zh, x, c = f(i // 8, (i // 2) % 4, i % 2)
        out.append((i, (zh % 2) * 8 + (x % 4) * 2 + c % 2))
    return out


def dp_perm(f):
    out = []
    for i in range(16):
        y, zl = f(i // 4, i % 4)
        out.append((i, (y % 4) * 4 + zl % 4))
    return out


C_SWAP = mp_perm(lambda zh, x, c: (zh, x, 1 - c))
ZH_SWAP = mp_perm(lambda zh, x, c: (1 - zh, x, c))


def X_TO(b):
    return mp_perm(lambda zh, x, c: (zh, x + b, c))


def Y_TO(b):
    return dp_perm(lambda y, zl: (y + b, zl))


def Z_XOR(b):
    return dp_perm(lambda y, zl: (y, zl ^ b))


def mp(v, perm):
    return lax.ppermute(v, "mp", perm)


def dp(v, perm):
    return lax.ppermute(v, "dp", perm)


def split(v):
    top = lax.reduce_precision(v, 8, 7)
    return top.astype(BF16), (v - top).astype(BF16)


def left3(v, axis):
    hi, lo = split(v)
    return jnp.concatenate([hi, lo, hi], axis=axis)


def right3(v, axis):
    hi, lo = split(v)
    return jnp.concatenate([hi, hi, lo], axis=axis)


def dot(a, b, ca, cb):
    return lax.dot_general(a, b, (((ca,), (cb,)), ((), ())), preferred_element_type=F32)


def reduce_mp(part, c):
    lo, hi = part[:, :768], part[:, 768:]
    send = jnp.where(c == 0, hi, lo)
    keep = jnp.where(c == 0, lo, hi)
    got = mp(send, C_SWAP)
    s = keep + got
    far, near = s[224:], s[:224]
    fb = [far[56 * b:56 * b + 56] for b in range(4)]
    nb = [near[56 * b:56 * b + 56] for b in range(4)]
    fr = [mp(fb[b], X_TO(b)) for b in (1, 3, 2)]
    nr = [mp(nb[b], X_TO(b)) for b in (1, 3, 2)]
    fs = fb[0] + fr[0] + fr[1] + fr[2]
    zr = mp(fs, ZH_SWAP)
    ns = nb[0] + nr[0] + nr[1] + nr[2]
    return ns + zr


def gather_mp(own, c, extra):
    n = 0 if extra is None else 8
    if n:
        own = jnp.concatenate([own, extra], axis=0)
    far = mp(own, ZH_SWAP)
    near_x = [own] + [mp(own, X_TO(-b)) for b in (1, 2, 3)]
    far_x = [far] + [mp(far, X_TO(-b)) for b in (1, 2, 3)]
    near = jnp.concatenate([v[:56] for v in near_x] + ([sum(v[56:] for v in near_x)] if n else []), axis=0)
    farr = jnp.concatenate([v[:56] for v in far_x] + ([sum(v[56:] for v in far_x)] if n else []), axis=0)
    near_o = mp(near, C_SWAP)
    far_o = mp(farr, C_SWAP)
    mine = jnp.concatenate([near[:224], farr[:224]], axis=0)
    other = jnp.concatenate([near_o[:224], far_o[:224]], axis=0)
    whole = jnp.concatenate([jnp.where(c == 0, mine, other), jnp.where(c == 0, other, mine)], axis=1)
    return whole, (near[224:] + farr[224:] + near_o[224:] + far_o[224:] if n else None)


def reduce_dp(blocks, zl, extra=None):
    if extra is not None:
        blocks = [jnp.concatenate([v, extra], axis=0) for v in blocks]
    got = [dp(blocks[b], Y_TO(b)) for b in (2, 1, 3)]
    s = blocks[0] + got[0] + got[1] + got[2]
    n = s.shape[0] // 4 // 8 * 8
    piece = [lax.dynamic_slice_in_dim(s, (zl ^ k) * n, n, 0) for k in range(4)]
    if extra is not None:
        piece = [jnp.concatenate([v, s[4 * n:]], axis=0) for v in piece]
    back = [dp(piece[k], Z_XOR(k)) for k in (2, 1, 3)]
    r = piece[0] + back[0] + back[1] + back[2]
    return r[:n], r[n:]


def body(frames, norm_gain, w_in, w_out, head_weight, teacher):
    m = lax.axis_index("mp")
    zh, x, c = m // 8, (m // 2) % 4, m % 2
    d = lax.axis_index("dp")
    y, zl = d // 4, d % 4

    w_in3 = right3(w_in, 0)
    w_out3 = right3(w_out, 0)
    w_outT3 = right3(w_out, 1)
    head3 = right3(head_weight[0], 0)
    headT3 = right3(head_weight[0], 1)

    far = mp(frames, ZH_SWAP)
    near_x = [frames] + [mp(frames, X_TO(-b)) for b in (1, 2, 3)]
    far_x = [far] + [mp(far, X_TO(-b)) for b in (1, 2, 3)]
    near = jnp.concatenate(near_x, axis=1)
    farr = jnp.concatenate(far_x, axis=1)
    near_o = mp(near, C_SWAP)
    far_o = mp(farr, C_SWAP)
    def half(mine, other):
        mine = mine.reshape(448, 4, 96)
        other = other.reshape(448, 4, 96)
        both = jnp.stack([jnp.where(c == 0, mine, other), jnp.where(c == 0, other, mine)], axis=2)
        both = both.reshape(448, 768)
        two = jnp.concatenate([both, both], axis=1)
        return lax.dynamic_slice_in_dim(two, ((4 - x) % 4) * 192, 768, 1)
    hn, hf = half(near, near_o), half(farr, far_o)
    canon = jnp.concatenate([jnp.where(zh == 0, hn, hf), jnp.where(zh == 0, hf, hn)], axis=1)
    target_c = teacher[0]
    starts = [((x + b) % 4) * 112 + (zh ^ a) * 56 for a in range(2) for b in range(4)]
    whole = jnp.concatenate([lax.dynamic_slice_in_dim(canon, s, 56, 0) for s in starts], axis=0)
    target = jnp.concatenate([lax.dynamic_slice_in_dim(target_c, s, 56, 0) for s in starts], axis=0)

    mean = jnp.mean(whole, axis=1, keepdims=True)
    centred = whole - mean
    var = jnp.mean(centred * centred, axis=1, keepdims=True)
    normed = centred * lax.rsqrt(var + 1e-05) * norm_gain
    normed3 = left3(normed, 1)
    normedT3 = left3(normed, 0)
    pre = dot(normed3, w_in3, 1, 0)
    sig = jax.nn.sigmoid(pre)
    act = pre * sig
    part = dot(left3(act, 1), w_out3, 1, 0)
    summed = reduce_mp(part, c)
    own = lax.dynamic_slice(whole, (0, c * 768), (56, 768)) + 0.5 * summed
    mixed, _ = gather_mp(own, c, None)

    codes = jnp.arange(1024, dtype=jnp.int32)
    logits = dot(left3(mixed, 1), head3, 1, 0)
    top = jnp.max(logits, axis=1, keepdims=True)
    expo = jnp.exp(logits - top)
    total = jnp.sum(expo, axis=1, keepdims=True)
    lse = top + jnp.log(total)
    onehot = (target[:, None] == codes[None, :]).astype(F32)
    picked = jnp.sum(logits * onehot, axis=1, keepdims=True)
    dlogits = expo / total - onehot
    local_loss = jnp.sum(lse - picked)
    dpartial = dot(left3(dlogits, 1), headT3, 1, 1)
    dlogits3 = right3(dlogits, 0)
    mixedT3 = left3(mixed, 0)
    gh_blocks = []
    for b in range(4):
        cols = lax.dynamic_slice_in_dim(mixedT3, ((y + b) % 4) * 384, 384, 1)
        gh_blocks.append(dot(cols, dlogits3, 0, 0))
    grad_head, _ = reduce_dp(gh_blocks, zl)
    dsum = reduce_mp(dpartial, c)
    dffn, loss_mp = gather_mp(0.5 * dsum, c, jnp.full((8, 768), local_loss, F32))

    act3 = right3(act, 0)
    dffnT3 = left3(dffn, 0)
    go_blocks = []
    for b in range(4):
        cols = lax.dynamic_slice_in_dim(dffnT3, ((y + b) % 4) * 384, 384, 1)
        go_blocks.append(dot(cols, act3, 0, 0))
    grad_outT, _ = reduce_dp(go_blocks, zl)
    dact = dot(left3(dffn, 1), w_outT3, 1, 1)
    dpre = dact * sig * (1.0 + pre * (1.0 - sig))
    dpre3 = right3(dpre, 0)
    gi_blocks = []
    for b in range(4):
        cols = lax.dynamic_slice_in_dim(normedT3, ((y + b) % 4) * 384, 384, 1)
        gi_blocks.append(dot(cols, dpre3, 0, 0))
    grad_in, loss_all = reduce_dp(gi_blocks, zl, loss_mp[:, :384])
    loss = loss_all[0, 0] / (7168 * 16)
    return (loss, grad_in, grad_outT.T, grad_head[None])


def solution(mesh):
    placed = (P("dp", "mp"), P(), P(None, "mp"), P("mp", None), P("mp", None, None), P("mp", "dp"))
    return jax.shard_map(
        body,
        mesh=mesh,
        in_specs=placed,
        out_specs=(P(), P("dp", "mp"), P("mp", "dp"), P("mp", "dp", None)),
        check_vma=False,
    )
```

```python
import jax
import jax.numpy as jnp
from jax import lax
from jax.experimental import pallas as pl
from jax.experimental.pallas import tpu as pltpu
from jax.sharding import PartitionSpec as P


F32 = jnp.float32
BF16 = jnp.bfloat16
ANY = pl.BlockSpec()
SMEM = pl.BlockSpec(memory_space=pltpu.SMEM)


def mp_perm(f):
    out = []
    for i in range(16):
        zh, x, c = f(i // 8, (i // 2) % 4, i % 2)
        out.append((i, (zh % 2) * 8 + (x % 4) * 2 + c % 2))
    return out


def dp_perm(f):
    out = []
    for i in range(16):
        y, zl = f(i // 4, i % 4)
        out.append((i, (y % 4) * 4 + zl % 4))
    return out


C_SWAP = mp_perm(lambda zh, x, c: (zh, x, 1 - c))
ZH_SWAP = mp_perm(lambda zh, x, c: (1 - zh, x, c))


def X_TO(b):
    return mp_perm(lambda zh, x, c: (zh, x + b, c))


def Y_TO(b):
    return dp_perm(lambda y, zl: (y + b, zl))


def Z_XOR(b):
    return dp_perm(lambda y, zl: (y, zl ^ b))


def mp(v, perm):
    return lax.ppermute(v, "mp", perm)


def dp(v, perm):
    return lax.ppermute(v, "dp", perm)


def split(v):
    top = lax.reduce_precision(v, 8, 7)
    return top.astype(BF16), (v - top).astype(BF16)


def left3(v, axis):
    hi, lo = split(v)
    return jnp.concatenate([hi, lo, hi], axis=axis)


def right3(v, axis):
    hi, lo = split(v)
    return jnp.concatenate([hi, hi, lo], axis=axis)


def pair3(hi, lo, axis):
    return jnp.concatenate([hi, hi, lo], axis=axis)


def dot(a, b, ca, cb):
    return lax.dot_general(a, b, (((ca,), (cb,)), ((), ())), preferred_element_type=F32)


def ksplit(v):
    hi = v.astype(BF16)
    return hi, (v - hi.astype(F32)).astype(BF16)


def kdot(a, b):
    return jnp.dot(a, b, preferred_element_type=F32)


def rows_of(zh, x, r):
    a, b = r // 4, r % 4
    z = zh if a == 0 else 1 - zh
    return pl.multiple_of(lax.rem(x + b, 4) * 112 + z * 56, 8)


def ffn_in_kernel(*refs):
    idx, fr = refs[0], refs[1]
    blocks, others = refs[2:10], refs[10:18]
    gain, whi, wlo, ohi, olo, nt_ref, send_ref, keep_ref, act_ref, pre_ref, actf, pref, both = refs[18:]
    zh, x, c = idx[0], idx[1], idx[2]
    src = []
    for r in range(8):
        z = zh if r < 4 else 1 - zh
        at = z * 8 + lax.rem(x + r % 4, 4) * 2
        src.append((at + c, blocks[r]))
        src.append((at + 1 - c, others[r]))
    total = jnp.zeros((1, 448), F32)
    for _, ref in src:
        total = total + jnp.sum(ref[...], axis=0, keepdims=True)
    mean = total * (1.0 / 1536.0)
    sq = jnp.zeros((1, 448), F32)
    for _, ref in src:
        v = ref[...] - mean
        sq = sq + jnp.sum(v * v, axis=0, keepdims=True)
    scale = lax.rsqrt(sq * (1.0 / 1536.0) + 1e-05)
    zero = jnp.zeros((1536, 64), BF16)
    for t in range(3):
        nt_ref[:, 512 * t + 448:512 * t + 512] = zero
    for at, ref in src:
        at = pl.multiple_of(at * 96, 32)
        v = (ref[...] - mean) * scale * gain[pl.ds(at, 96), :]
        hi, lo = ksplit(v)
        nt_ref[pl.ds(at, 96), 0:448] = hi
        nt_ref[pl.ds(at, 96), 512:960] = lo
        nt_ref[pl.ds(at, 96), 1024:1472] = hi
    hi, lo = nt_ref[:, 0:512], nt_ref[:, 512:1024]
    pre = (kdot(whi[...], hi) + kdot(wlo[...], hi) + kdot(whi[...], lo)).T
    pref[...] = pre
    actf[:, 0:384] = 0.5 * (pre * jax.nn.sigmoid(pre))
    actf[0:448, 384:480] = fr[...]
    actf[:, 480:512] = jnp.zeros((512, 32), F32)
    for i in range(4):
        s0, s1 = rows_of(zh, x, 2 * i), rows_of(zh, x, 2 * i + 1)
        v = jnp.concatenate([actf[pl.ds(s0, 56), :], actf[pl.ds(s1, 56), :]], axis=0)
        hi, lo = ksplit(v)
        at = 112 * i
        both[at:at + 112, :] = hi
        both[at + 448:at + 560, :] = lo
        for t, q in ((0, hi), (1, hi), (2, lo)):
            act_ref[448 * t + at:448 * t + at + 112, :] = q[:, 0:384]
        pre_ref[at:at + 56, :] = pref[pl.ds(s0, 56), :]
        pre_ref[at + 56:at + 112, :] = pref[pl.ds(s1, 56), :]
    own = zh * 8 + x * 2 + c
    row = lax.broadcasted_iota(jnp.int32, (128, 768), 0)
    col = lax.broadcasted_iota(jnp.int32, (128, 768), 1)
    for ref, half in ((send_ref, 1 - c), (keep_ref, c)):
        pick = jnp.where((row + own * 96 - half * 768 == col) & (row < 96), 1.0, 0.0).astype(BF16)
        cols = pl.ds(pl.multiple_of(half * 768, 128), 768)
        p = kdot(both[...], jnp.concatenate([ohi[:, cols], pick], axis=0))
        ref[...] = p[0:448] + p[448:896] + kdot(both[0:448, 0:384], olo[:, cols])


def ffn_in(*args):
    return pl.pallas_call(
        ffn_in_kernel,
        out_shape=(
            jax.ShapeDtypeStruct((1536, 1536), BF16),
            jax.ShapeDtypeStruct((448, 768), F32),
            jax.ShapeDtypeStruct((448, 768), F32),
            jax.ShapeDtypeStruct((1344, 384), BF16),
            jax.ShapeDtypeStruct((448, 384), F32),
        ),
        in_specs=[SMEM] + [ANY] * 22,
        out_specs=(ANY,) * 5,
        scratch_shapes=[pltpu.VMEM((512, 512), F32), pltpu.VMEM((512, 384), F32), pltpu.VMEM((896, 512), BF16)],
        compiler_params=pltpu.CompilerParams(vmem_limit_bytes=56 << 20),
        name="ffn_in",
    )(*args)


def join_kernel(*refs):
    idx, mine, other, row_ref, col_ref = refs[0], refs[1:9], refs[9:17], refs[17], refs[18]
    c = idx[2]
    for i in range(4):
        at = 112 * i
        for o, g in ((c, mine), (1 - c, other)):
            hi, lo = ksplit(jnp.concatenate([g[2 * i][0:56, :], g[2 * i + 1][0:56, :]], axis=0))
            for t, q in ((0, hi), (1, lo), (2, hi)):
                row_ref[at:at + 112, pl.ds(pl.multiple_of(1536 * t + o * 768, 128), 768)] = q
                col_ref[448 * t + at:448 * t + at + 112, pl.ds(pl.multiple_of(o * 768, 128), 768)] = q


def join(idx, mine, other):
    return pl.pallas_call(
        join_kernel,
        out_shape=(jax.ShapeDtypeStruct((448, 4608), BF16), jax.ShapeDtypeStruct((1344, 1536), BF16)),
        in_specs=[SMEM] + [ANY] * 16,
        out_specs=(ANY, ANY),
        compiler_params=pltpu.CompilerParams(vmem_limit_bytes=40 << 20),
        name="join",
    )(idx, *mine, *other)


def dpre_kernel(idx, da, pre_ref, out_ref):
    zh, x = idx[0], idx[1]
    zero = jnp.zeros((64, 384), BF16)
    for t in range(3):
        out_ref[512 * t + 448:512 * t + 512, :] = zero
    for i in range(4):
        at = pl.multiple_of(lax.rem(i - x + 4, 4) * 56, 8)
        res = []
        for o in (0, 224):
            p, g = pre_ref[pl.ds(at + o, 56), :], da[pl.ds(at + o, 56), :]
            s = jax.nn.sigmoid(p)
            res.append((0.5 * g) * s * (1.0 + p * (1.0 - s)))
        flip = zh == 1
        first = jnp.where(flip, res[1], res[0])
        second = jnp.where(flip, res[0], res[1])
        hi, lo = ksplit(jnp.concatenate([first, second], axis=0))
        for t, q in ((0, hi), (1, hi), (2, lo)):
            out_ref[512 * t + 112 * i:512 * t + 112 * i + 112, :] = q


def dpre_of(idx, da, pre):
    return pl.pallas_call(
        dpre_kernel,
        out_shape=jax.ShapeDtypeStruct((1536, 384), BF16),
        in_specs=[SMEM] + [ANY] * 2,
        out_specs=ANY,
        name="dpre",
    )(idx, da, pre)


def reduce_x(s):
    blk = [s[56 * b:56 * b + 56] for b in range(4)]
    got = [mp(blk[b], X_TO(b)) for b in (2, 1, 3)]
    return blk[0] + got[0] + got[1] + got[2]


def gather_blocks(own):
    far = mp(own, ZH_SWAP)
    mine = [own] + [mp(own, X_TO(-b)) for b in (1, 2, 3)]
    mine += [far] + [mp(far, X_TO(-b)) for b in (1, 2, 3)]
    return mine, [mp(v, C_SWAP) for v in mine]


def reduce_mp(send, keep):
    s = keep + mp(send, C_SWAP)
    fs = reduce_x(s[224:])
    zr = mp(fs, ZH_SWAP)
    return reduce_x(s[:224]) + zr


def ring_y(v, y, gate, extra=None):
    def rows(w, b, o, n):
        r = lax.dynamic_slice_in_dim(w, lax.rem(y + b, 4) * 384 + o, n, 0)
        return r if extra is None or o + n < 384 else jnp.concatenate([r, extra], axis=0)

    top, bot, w = lax.optimization_barrier((rows(v, 2, 0, 192), rows(v, 2, 192, 192), v))
    u, d = dp(top, Y_TO(1)), dp(bot, Y_TO(-1))
    w, _ = lax.optimization_barrier((w, gate))
    p = jnp.concatenate([rows(w, 1, 0, 192) + u, rows(w, 1, 192, 192)], axis=0)
    p = lax.optimization_barrier(p)
    q = jnp.concatenate([rows(w, 3, 0, 192), rows(w, 3, 192, 192) + d], axis=0)
    q = lax.optimization_barrier(q)
    p, q = dp(p, Y_TO(1)), dp(q, Y_TO(-1))
    return rows(w, 0, 0, 384) + p + q


def line_z(v, zl, tail=0):
    def piece(k):
        r = lax.dynamic_slice_in_dim(v, (zl ^ k) * 96, 96, 0)
        return jnp.concatenate([r, v[384:]], axis=0) if tail else r

    back = [dp(piece(k), Z_XOR(k)) for k in (2, 1, 3)]
    return piece(0) + back[0] + back[1] + back[2]


def step(frames, norm_gain, w_in, w_out, head_weight, teacher):
    m = lax.axis_index("mp")
    zh, x, c = m // 8, (m // 2) % 4, m % 2
    d = lax.axis_index("dp")
    y, zl = d // 4, d % 4
    idx = jnp.stack([zh, x, c]).astype(jnp.int32)

    mine, other = gather_blocks(frames.T)

    whi, wlo = split(w_in.T)
    ohi, olo = split(w_out)
    hhi, hlo = split(head_weight[0])
    gain = norm_gain.reshape(1536, 1)
    starts = [((x + b) % 4) * 112 + (zh ^ a) * 56 for a in range(2) for b in range(4)]
    target = jnp.concatenate([lax.dynamic_slice_in_dim(teacher[0], s, 56, 0) for s in starts], axis=0)
    other[0], whi, wlo, ohi, olo, hhi, hlo, gain, target = lax.optimization_barrier(
        (other[0], whi, wlo, ohi, olo, hhi, hlo, gain, target))

    nt, send, keep, act3, pre = ffn_in(idx, frames, *mine, *other, gain, whi, wlo, ohi, olo)
    mine, other = gather_blocks(reduce_mp(send, keep))
    row3, col3 = join(idx, mine, other)

    codes = jnp.arange(1024, dtype=jnp.int32)
    logits = dot(row3, pair3(hhi, hlo, 0), 1, 0)
    top = jnp.max(logits, axis=1, keepdims=True)
    expo = jnp.exp(logits - top)
    total = jnp.sum(expo, axis=1, keepdims=True)
    lse = top + jnp.log(total)
    onehot = (target[:, None] == codes[None, :]).astype(F32)
    picked = jnp.sum(logits * onehot, axis=1, keepdims=True)
    dlogits = expo / total - onehot
    extra = jnp.full((8, 768), jnp.sum(lse - picked), F32)
    part = dot(left3(dlogits, 1), pair3(hhi, hlo, 1), 1, 1)
    send = lax.dynamic_slice_in_dim(part, (1 - c) * 768, 768, 1)
    keep = lax.dynamic_slice_in_dim(part, c * 768, 768, 1)

    gh = dot(col3, right3(dlogits, 0), 0, 0)
    own = reduce_mp(send, keep)
    gs = ring_y(gh, y, own)
    grad_head = line_z(gs, zl)
    mine, other = gather_blocks(jnp.concatenate([own, extra], axis=0))
    row3, col3 = join(idx, mine, other)
    loss_mp = sum(v[56:, :384] for v in mine + other)

    go = dot(col3, act3, 0, 0)
    da = dot(row3, pair3(ohi, olo, 1), 1, 1)
    dpre3 = dpre_of(idx, da, pre)
    gi = dot(nt, dpre3, 1, 0)
    grad_outT = line_z(ring_y(go, y, gi), zl)
    r = line_z(ring_y(gi, y, go, loss_mp), zl, 8)
    loss = r[96, 0] / (7168 * 16)
    return (loss, r[:96], grad_outT.T, grad_head[None])


def solution(mesh):
    placed = (P("dp", "mp"), P(), P(None, "mp"), P("mp", None), P("mp", None, None), P("mp", "dp"))
    return jax.shard_map(
        step,
        mesh=mesh,
        in_specs=placed,
        out_specs=(P(), P("dp", "mp"), P("mp", "dp"), P("mp", "dp", None)),
        check_vma=False,
    )
```

```python
import jax
import jax.numpy as jnp
from jax import lax
from jax.experimental import pallas as pl
from jax.experimental.pallas import tpu as pltpu
from jax.sharding import PartitionSpec as P


F32 = jnp.float32
BF16 = jnp.bfloat16
ANY = pl.BlockSpec()
SMEM = pl.BlockSpec(memory_space=pltpu.SMEM)


def mp_perm(f):
    out = []
    for i in range(16):
        zh, x, c = f(i // 8, (i // 2) % 4, i % 2)
        out.append((i, (zh % 2) * 8 + (x % 4) * 2 + c % 2))
    return out


def dp_perm(f):
    out = []
    for i in range(16):
        y, zl = f(i // 4, i % 4)
        out.append((i, (y % 4) * 4 + zl % 4))
    return out


C_SWAP = mp_perm(lambda zh, x, c: (zh, x, 1 - c))
ZH_SWAP = mp_perm(lambda zh, x, c: (1 - zh, x, c))


def X_TO(b):
    return mp_perm(lambda zh, x, c: (zh, x + b, c))


def Y_TO(b):
    return dp_perm(lambda y, zl: (y + b, zl))


def Z_XOR(b):
    return dp_perm(lambda y, zl: (y, zl ^ b))


def mp(v, perm):
    return lax.ppermute(v, "mp", perm)


def dp(v, perm):
    return lax.ppermute(v, "dp", perm)


def split(v):
    top = lax.reduce_precision(v, 8, 7)
    return top.astype(BF16), (v - top).astype(BF16)


def left3(v, axis):
    hi, lo = split(v)
    return jnp.concatenate([hi, lo, hi], axis=axis)


def right3(v, axis):
    hi, lo = split(v)
    return jnp.concatenate([hi, hi, lo], axis=axis)


def pair3(hi, lo, axis):
    return jnp.concatenate([hi, hi, lo], axis=axis)


def dot(a, b, ca, cb):
    return lax.dot_general(a, b, (((ca,), (cb,)), ((), ())), preferred_element_type=F32)


def ksplit(v):
    hi = v.astype(BF16)
    return hi, (v - hi.astype(F32)).astype(BF16)


def kdot(a, b):
    return jnp.dot(a, b, preferred_element_type=F32)


def rows_of(zh, x, r):
    a, b = r // 4, r % 4
    z = zh if a == 0 else 1 - zh
    return pl.multiple_of(lax.rem(x + b, 4) * 112 + z * 56, 8)


def ffn_in_kernel(*refs):
    idx, fr = refs[0], refs[1]
    blocks, others = refs[2:10], refs[10:18]
    gain, whi, wlo, ohi, olo, nt_ref, send_ref, keep_ref, act_ref, pre_ref, actf, pref, both = refs[18:]
    zh, x, c = idx[0], idx[1], idx[2]
    src = []
    for r in range(8):
        z = zh if r < 4 else 1 - zh
        at = z * 8 + lax.rem(x + r % 4, 4) * 2
        src.append((at + c, blocks[r]))
        src.append((at + 1 - c, others[r]))
    total = jnp.zeros((1, 448), F32)
    for _, ref in src:
        total = total + jnp.sum(ref[...], axis=0, keepdims=True)
    mean = total * (1.0 / 1536.0)
    sq = jnp.zeros((1, 448), F32)
    for _, ref in src:
        v = ref[...] - mean
        sq = sq + jnp.sum(v * v, axis=0, keepdims=True)
    scale = lax.rsqrt(sq * (1.0 / 1536.0) + 1e-05)
    zero = jnp.zeros((1536, 64), BF16)
    for t in range(3):
        nt_ref[:, 512 * t + 448:512 * t + 512] = zero
    for at, ref in src:
        at = pl.multiple_of(at * 96, 32)
        v = (ref[...] - mean) * scale * gain[pl.ds(at, 96), :]
        hi, lo = ksplit(v)
        nt_ref[pl.ds(at, 96), 0:448] = hi
        nt_ref[pl.ds(at, 96), 512:960] = lo
        nt_ref[pl.ds(at, 96), 1024:1472] = hi
    hi, lo = nt_ref[:, 0:512], nt_ref[:, 512:1024]
    pre = (kdot(whi[...], hi) + kdot(wlo[...], hi) + kdot(whi[...], lo)).T
    pref[...] = pre
    actf[:, 0:384] = 0.5 * (pre * jax.nn.sigmoid(pre))
    actf[0:448, 384:480] = fr[...]
    actf[:, 480:512] = jnp.zeros((512, 32), F32)
    for i in range(4):
        s0, s1 = rows_of(zh, x, 2 * i), rows_of(zh, x, 2 * i + 1)
        v = jnp.concatenate([actf[pl.ds(s0, 56), :], actf[pl.ds(s1, 56), :]], axis=0)
        hi, lo = ksplit(v)
        at = 112 * i
        both[at:at + 112, :] = hi
        both[at + 448:at + 560, :] = lo
        for t, q in ((0, hi), (1, hi), (2, lo)):
            act_ref[448 * t + at:448 * t + at + 112, :] = q[:, 0:384]
        pre_ref[at:at + 56, :] = pref[pl.ds(s0, 56), :]
        pre_ref[at + 56:at + 112, :] = pref[pl.ds(s1, 56), :]
    own = zh * 8 + x * 2 + c
    row = lax.broadcasted_iota(jnp.int32, (128, 768), 0)
    col = lax.broadcasted_iota(jnp.int32, (128, 768), 1)
    for ref, half in ((send_ref, 1 - c), (keep_ref, c)):
        pick = jnp.where((row + own * 96 - half * 768 == col) & (row < 96), 1.0, 0.0).astype(BF16)
        cols = pl.ds(pl.multiple_of(half * 768, 128), 768)
        p = kdot(both[...], jnp.concatenate([ohi[:, cols], pick], axis=0))
        ref[...] = p[0:448] + p[448:896] + kdot(both[0:448, 0:384], olo[:, cols])


def ffn_in(*args):
    return pl.pallas_call(
        ffn_in_kernel,
        out_shape=(
            jax.ShapeDtypeStruct((1536, 1536), BF16),
            jax.ShapeDtypeStruct((448, 768), F32),
            jax.ShapeDtypeStruct((448, 768), F32),
            jax.ShapeDtypeStruct((1344, 384), BF16),
            jax.ShapeDtypeStruct((448, 384), F32),
        ),
        in_specs=[SMEM] + [ANY] * 22,
        out_specs=(ANY,) * 5,
        scratch_shapes=[pltpu.VMEM((512, 512), F32), pltpu.VMEM((512, 384), F32), pltpu.VMEM((896, 512), BF16)],
        compiler_params=pltpu.CompilerParams(vmem_limit_bytes=56 << 20),
        name="ffn_in",
    )(*args)


def join_kernel(*refs):
    idx, mine, other, row_ref, col_ref = refs[0], refs[1:9], refs[9:17], refs[17], refs[18]
    c = idx[2]
    for i in range(4):
        at = 112 * i
        for o, g in ((c, mine), (1 - c, other)):
            hi, lo = ksplit(jnp.concatenate([g[2 * i][0:56, :], g[2 * i + 1][0:56, :]], axis=0))
            for t, q in ((0, hi), (1, lo), (2, hi)):
                row_ref[at:at + 112, pl.ds(pl.multiple_of(1536 * t + o * 768, 128), 768)] = q
                col_ref[448 * t + at:448 * t + at + 112, pl.ds(pl.multiple_of(o * 768, 128), 768)] = q


def join(idx, mine, other):
    return pl.pallas_call(
        join_kernel,
        out_shape=(jax.ShapeDtypeStruct((448, 4608), BF16), jax.ShapeDtypeStruct((1344, 1536), BF16)),
        in_specs=[SMEM] + [ANY] * 16,
        out_specs=(ANY, ANY),
        compiler_params=pltpu.CompilerParams(vmem_limit_bytes=40 << 20),
        name="join",
    )(idx, *mine, *other)


def dpre_kernel(idx, da, pre_ref, out_ref):
    zh, x = idx[0], idx[1]
    zero = jnp.zeros((64, 384), BF16)
    for t in range(3):
        out_ref[512 * t + 448:512 * t + 512, :] = zero
    for i in range(4):
        at = pl.multiple_of(lax.rem(i - x + 4, 4) * 56, 8)
        res = []
        for o in (0, 224):
            p, g = pre_ref[pl.ds(at + o, 56), :], da[pl.ds(at + o, 56), :]
            s = jax.nn.sigmoid(p)
            res.append((0.5 * g) * s * (1.0 + p * (1.0 - s)))
        flip = zh == 1
        first = jnp.where(flip, res[1], res[0])
        second = jnp.where(flip, res[0], res[1])
        hi, lo = ksplit(jnp.concatenate([first, second], axis=0))
        for t, q in ((0, hi), (1, hi), (2, lo)):
            out_ref[512 * t + 112 * i:512 * t + 112 * i + 112, :] = q


def dpre_of(idx, da, pre):
    return pl.pallas_call(
        dpre_kernel,
        out_shape=jax.ShapeDtypeStruct((1536, 384), BF16),
        in_specs=[SMEM] + [ANY] * 2,
        out_specs=ANY,
        name="dpre",
    )(idx, da, pre)


def reduce_x(s):
    blk = [s[56 * b:56 * b + 56] for b in range(4)]
    got = [mp(blk[b], X_TO(b)) for b in (2, 1, 3)]
    return blk[0] + got[0] + got[1] + got[2]


def gather_blocks(own):
    far = mp(own, ZH_SWAP)
    mine = [own] + [mp(own, X_TO(-b)) for b in (1, 2, 3)]
    mine += [far] + [mp(far, X_TO(-b)) for b in (1, 2, 3)]
    return mine, [mp(v, C_SWAP) for v in mine]


def reduce_mp(send, keep):
    s = keep + mp(send, C_SWAP)
    fs = reduce_x(s[224:])
    zr = mp(fs, ZH_SWAP)
    return reduce_x(s[:224]) + zr


def ring_y(v, y, gate, extra=None):
    def top(w, b):
        return lax.dynamic_slice_in_dim(w, lax.rem(y + b, 4) * 384, 192, 0)

    def bot(w, b):
        r = lax.dynamic_slice_in_dim(w, lax.rem(y + b, 4) * 384 + 192, 192, 0)
        return r if extra is None else jnp.concatenate([r, extra], axis=0)

    t2, b2, b1, t3, w = lax.optimization_barrier((top(v, 2), bot(v, 2), bot(v, 1), top(v, 3), v))
    u, d = dp(t2, Y_TO(1)), dp(b2, Y_TO(-1))
    b1, t3 = dp(b1, Y_TO(1)), dp(t3, Y_TO(-1))
    w, _ = lax.optimization_barrier((w, gate))
    p = dp(lax.optimization_barrier(top(w, 1) + u), Y_TO(1))
    q = dp(lax.optimization_barrier(bot(w, 3) + d), Y_TO(-1))
    t3, b1, p, q, w = lax.optimization_barrier((t3, b1, p, q, w))
    return jnp.concatenate([top(w, 0) + t3 + p, bot(w, 0) + b1 + q], axis=0)


def line_z(v, zl, tail=0):
    def piece(k):
        r = lax.dynamic_slice_in_dim(v, (zl ^ k) * 96, 96, 0)
        return jnp.concatenate([r, v[384:]], axis=0) if tail else r

    n = 96 + tail
    both, w = lax.optimization_barrier((jnp.concatenate([piece(3), piece(1)], axis=0), v))
    got = dp(both, Z_XOR(1))
    v = w
    on = dp(piece(2) + got[:n], Z_XOR(2))
    return piece(0) + got[n:] + on


def split_kernel(w, hi, lo):
    hi[...], lo[...] = ksplit(w[...])


def split_rows(w):
    n, m = w.shape
    blk = pl.BlockSpec((n // 8, m), lambda i: (i, 0))
    return pl.pallas_call(
        split_kernel,
        grid=(8,),
        out_shape=(jax.ShapeDtypeStruct((n, m), BF16),) * 2,
        in_specs=[blk],
        out_specs=(blk, blk),
        name="split_rows",
    )(w)


def step(frames, norm_gain, w_in, w_out, head_weight, teacher):
    m = lax.axis_index("mp")
    zh, x, c = m // 8, (m // 2) % 4, m % 2
    d = lax.axis_index("dp")
    y, zl = d // 4, d % 4
    idx = jnp.stack([zh, x, c]).astype(jnp.int32)

    mine, other = gather_blocks(frames.T)

    whi, wlo = split(w_in.T)
    ohi, olo = split(w_out)
    hhi, hlo = split_rows(head_weight[0])
    gain = norm_gain.reshape(1536, 1)
    starts = [((x + b) % 4) * 112 + (zh ^ a) * 56 for a in range(2) for b in range(4)]
    target = jnp.concatenate([lax.dynamic_slice_in_dim(teacher[0], s, 56, 0) for s in starts], axis=0)
    other[0], whi, wlo, ohi, olo, gain, target = lax.optimization_barrier(
        (other[0], whi, wlo, ohi, olo, gain, target))

    nt, send, keep, act3, pre = ffn_in(idx, frames, *mine, *other, gain, whi, wlo, ohi, olo)
    mine, other = gather_blocks(reduce_mp(send, keep))
    row3, col3 = join(idx, mine, other)

    codes = jnp.arange(1024, dtype=jnp.int32)
    logits = dot(row3, pair3(hhi, hlo, 0), 1, 0)
    top = jnp.max(logits, axis=1, keepdims=True)
    expo = jnp.exp(logits - top)
    total = jnp.sum(expo, axis=1, keepdims=True)
    lse = top + jnp.log(total)
    onehot = (target[:, None] == codes[None, :]).astype(F32)
    picked = jnp.sum(logits * onehot, axis=1, keepdims=True)
    dlogits = expo / total - onehot
    extra = jnp.full((8, 768), jnp.sum(lse - picked), F32)
    part = dot(left3(dlogits, 1), pair3(hhi, hlo, 1), 1, 1)
    send = lax.dynamic_slice_in_dim(part, (1 - c) * 768, 768, 1)
    keep = lax.dynamic_slice_in_dim(part, c * 768, 768, 1)

    gh = dot(col3, right3(dlogits, 0), 0, 0)
    own = reduce_mp(send, keep)
    mine, other = gather_blocks(jnp.concatenate([own, extra], axis=0))
    gs = ring_y(gh, y, tuple(mine[1:4]))
    grad_head = line_z(gs, zl)
    row3, col3 = join(idx, mine, other)
    loss_mp = sum(v[56:, :384] for v in mine + other)

    go = dot(col3, act3, 0, 0)
    da = dot(row3, pair3(ohi, olo, 1), 1, 1)
    dpre3 = dpre_of(idx, da, pre)
    gi = dot(nt, dpre3, 1, 0)
    grad_outT = line_z(ring_y(go, y, gi), zl)
    r = line_z(ring_y(gi, y, go, loss_mp), zl, 8)
    loss = r[96, 0] / (7168 * 16)
    return (loss, r[:96], grad_outT.T, grad_head[None])


def solution(mesh):
    placed = (P("dp", "mp"), P(), P(None, "mp"), P("mp", None), P("mp", None, None), P("mp", "dp"))
    return jax.shard_map(
        step,
        mesh=mesh,
        in_specs=placed,
        out_specs=(P(), P("dp", "mp"), P("mp", "dp"), P("mp", "dp", None)),
        check_vma=False,
    )
```

```python
import jax
import jax.numpy as jnp
from jax import lax
from jax.experimental import pallas as pl
from jax.experimental.pallas import tpu as pltpu
from jax.sharding import PartitionSpec as P


F32 = jnp.float32
BF16 = jnp.bfloat16
ANY = pl.BlockSpec()
SMEM = pl.BlockSpec(memory_space=pltpu.SMEM)


def mp_perm(f):
    out = []
    for i in range(16):
        zh, x, c = f(i // 8, (i // 2) % 4, i % 2)
        out.append((i, (zh % 2) * 8 + (x % 4) * 2 + c % 2))
    return out


def dp_perm(f):
    out = []
    for i in range(16):
        y, zl = f(i // 4, i % 4)
        out.append((i, (y % 4) * 4 + zl % 4))
    return out


C_SWAP = mp_perm(lambda zh, x, c: (zh, x, 1 - c))
ZH_SWAP = mp_perm(lambda zh, x, c: (1 - zh, x, c))


def X_TO(b):
    return mp_perm(lambda zh, x, c: (zh, x + b, c))


def Y_TO(b):
    return dp_perm(lambda y, zl: (y + b, zl))


def Z_XOR(b):
    return dp_perm(lambda y, zl: (y, zl ^ b))


def mp(v, perm):
    return lax.ppermute(v, "mp", perm)


def dp(v, perm):
    return lax.ppermute(v, "dp", perm)


def split(v):
    top = lax.reduce_precision(v, 8, 7)
    return top.astype(BF16), (v - top).astype(BF16)


def left3(v, axis):
    hi, lo = split(v)
    return jnp.concatenate([hi, lo, hi], axis=axis)


def right3(v, axis):
    hi, lo = split(v)
    return jnp.concatenate([hi, hi, lo], axis=axis)


def pair3(hi, lo, axis):
    return jnp.concatenate([hi, hi, lo], axis=axis)


def dot(a, b, ca, cb):
    return lax.dot_general(a, b, (((ca,), (cb,)), ((), ())), preferred_element_type=F32)


def ksplit(v):
    hi = v.astype(BF16)
    return hi, (v - hi.astype(F32)).astype(BF16)


def kdot(a, b):
    return jnp.dot(a, b, preferred_element_type=F32)


def rows_of(zh, x, r):
    a, b = r // 4, r % 4
    z = zh if a == 0 else 1 - zh
    return pl.multiple_of(lax.rem(x + b, 4) * 112 + z * 56, 8)


def ffn_in_kernel(*refs):
    idx, fr = refs[0], refs[1]
    blocks, others = refs[2:10], refs[10:18]
    whi, wlo, ohi, olo, nt_ref, send_ref, keep_ref, act_ref, pre_ref, actf, pref, both = refs[18:]
    zh, x, c = idx[0], idx[1], idx[2]
    src = []
    for r in range(8):
        z = zh if r < 4 else 1 - zh
        at = z * 8 + lax.rem(x + r % 4, 4) * 2
        src.append((at + c, blocks[r]))
        src.append((at + 1 - c, others[r]))
    total = jnp.zeros((1, 448), F32)
    for _, ref in src:
        total = total + jnp.sum(ref[...], axis=0, keepdims=True)
    mean = total * (1.0 / 1536.0)
    sq = jnp.zeros((1, 448), F32)
    for _, ref in src:
        v = ref[...] - mean
        sq = sq + jnp.sum(v * v, axis=0, keepdims=True)
    scale = lax.rsqrt(sq * (1.0 / 1536.0) + 1e-05)
    zero = jnp.zeros((1536, 64), BF16)
    for t in range(3):
        nt_ref[:, 512 * t + 448:512 * t + 512] = zero
    for at, ref in src:
        at = pl.multiple_of(at * 96, 32)
        v = (ref[...] - mean) * scale
        hi, lo = ksplit(v)
        nt_ref[pl.ds(at, 96), 0:448] = hi
        nt_ref[pl.ds(at, 96), 512:960] = lo
        nt_ref[pl.ds(at, 96), 1024:1472] = hi
    hi, lo = nt_ref[:, 0:512], nt_ref[:, 512:1024]
    pre = (kdot(whi[...], hi) + kdot(wlo[...], hi) + kdot(whi[...], lo)).T
    pref[...] = pre
    actf[:, 0:384] = 0.5 * (pre * jax.nn.sigmoid(pre))
    actf[0:448, 384:480] = fr[...]
    actf[:, 480:512] = jnp.zeros((512, 32), F32)
    for i in range(4):
        s0, s1 = rows_of(zh, x, 2 * i), rows_of(zh, x, 2 * i + 1)
        v = jnp.concatenate([actf[pl.ds(s0, 56), :], actf[pl.ds(s1, 56), :]], axis=0)
        hi, lo = ksplit(v)
        at = 112 * i
        both[at:at + 112, :] = hi
        both[at + 448:at + 560, :] = lo
        for t, q in ((0, hi), (1, hi), (2, lo)):
            act_ref[448 * t + at:448 * t + at + 112, :] = q[:, 0:384]
        pre_ref[at:at + 56, :] = pref[pl.ds(s0, 56), :]
        pre_ref[at + 56:at + 112, :] = pref[pl.ds(s1, 56), :]
    own = zh * 8 + x * 2 + c
    row = lax.broadcasted_iota(jnp.int32, (128, 768), 0)
    col = lax.broadcasted_iota(jnp.int32, (128, 768), 1)
    for ref, half in ((send_ref, 1 - c), (keep_ref, c)):
        pick = jnp.where((row + own * 96 - half * 768 == col) & (row < 96), 1.0, 0.0).astype(BF16)
        cols = pl.ds(pl.multiple_of(half * 768, 128), 768)
        p = kdot(both[...], jnp.concatenate([ohi[:, cols], pick], axis=0))
        ref[...] = p[0:448] + p[448:896] + kdot(both[0:448, 0:384], olo[:, cols])


def ffn_in(*args):
    return pl.pallas_call(
        ffn_in_kernel,
        out_shape=(
            jax.ShapeDtypeStruct((1536, 1536), BF16),
            jax.ShapeDtypeStruct((448, 768), F32),
            jax.ShapeDtypeStruct((448, 768), F32),
            jax.ShapeDtypeStruct((1344, 384), BF16),
            jax.ShapeDtypeStruct((448, 384), F32),
        ),
        in_specs=[SMEM] + [ANY] * 21,
        out_specs=(ANY,) * 5,
        scratch_shapes=[pltpu.VMEM((512, 512), F32), pltpu.VMEM((512, 384), F32), pltpu.VMEM((896, 512), BF16)],
        compiler_params=pltpu.CompilerParams(vmem_limit_bytes=56 << 20),
        name="ffn_in",
    )(*args)


def join_kernel(*refs):
    idx, mine, other, row_ref, col_ref = refs[0], refs[1:9], refs[9:17], refs[17], refs[18]
    c = idx[2]
    for i in range(4):
        at = 112 * i
        for o, g in ((c, mine), (1 - c, other)):
            hi, lo = ksplit(jnp.concatenate([g[2 * i][0:56, :], g[2 * i + 1][0:56, :]], axis=0))
            for t, q in ((0, hi), (1, lo), (2, hi)):
                row_ref[at:at + 112, pl.ds(pl.multiple_of(1536 * t + o * 768, 128), 768)] = q
                col_ref[448 * t + at:448 * t + at + 112, pl.ds(pl.multiple_of(o * 768, 128), 768)] = q


def join(idx, mine, other):
    return pl.pallas_call(
        join_kernel,
        out_shape=(jax.ShapeDtypeStruct((448, 4608), BF16), jax.ShapeDtypeStruct((1344, 1536), BF16)),
        in_specs=[SMEM] + [ANY] * 16,
        out_specs=(ANY, ANY),
        compiler_params=pltpu.CompilerParams(vmem_limit_bytes=40 << 20),
        name="join",
    )(idx, *mine, *other)


def dpre_kernel(idx, da, pre_ref, out_ref):
    zh, x = idx[0], idx[1]
    zero = jnp.zeros((64, 384), BF16)
    for t in range(3):
        out_ref[512 * t + 448:512 * t + 512, :] = zero
    for i in range(4):
        at = pl.multiple_of(lax.rem(i - x + 4, 4) * 56, 8)
        res = []
        for o in (0, 224):
            p, g = pre_ref[pl.ds(at + o, 56), :], da[pl.ds(at + o, 56), :]
            s = jax.nn.sigmoid(p)
            res.append((0.5 * g) * s * (1.0 + p * (1.0 - s)))
        flip = zh == 1
        first = jnp.where(flip, res[1], res[0])
        second = jnp.where(flip, res[0], res[1])
        hi, lo = ksplit(jnp.concatenate([first, second], axis=0))
        for t, q in ((0, hi), (1, hi), (2, lo)):
            out_ref[512 * t + 112 * i:512 * t + 112 * i + 112, :] = q


def dpre_of(idx, da, pre):
    return pl.pallas_call(
        dpre_kernel,
        out_shape=jax.ShapeDtypeStruct((1536, 384), BF16),
        in_specs=[SMEM] + [ANY] * 2,
        out_specs=ANY,
        name="dpre",
    )(idx, da, pre)


def reduce_x(s):
    blk = [s[56 * b:56 * b + 56] for b in range(4)]
    got = [mp(blk[b], X_TO(b)) for b in (2, 1, 3)]
    return blk[0] + got[0] + got[1] + got[2]


def gather_blocks(own):
    far = mp(own, ZH_SWAP)
    mine = [own] + [mp(own, X_TO(-b)) for b in (1, 2, 3)]
    mine += [far] + [mp(far, X_TO(-b)) for b in (1, 2, 3)]
    return mine, [mp(v, C_SWAP) for v in mine]


def reduce_mp(send, keep):
    s = keep + mp(send, C_SWAP)
    fs = reduce_x(s[224:])
    zr = mp(fs, ZH_SWAP)
    return reduce_x(s[:224]) + zr


def ring_y(v, y, gate, extra=None):
    def top(w, b):
        return lax.dynamic_slice_in_dim(w, lax.rem(y + b, 4) * 384, 192, 0)

    def bot(w, b):
        r = lax.dynamic_slice_in_dim(w, lax.rem(y + b, 4) * 384 + 192, 192, 0)
        return r if extra is None else jnp.concatenate([r, extra], axis=0)

    cuts = (top(v, 2), bot(v, 2), bot(v, 1), top(v, 3))
    t2, b2, b1, t3, w = lax.optimization_barrier((*cuts, v))
    u, d = dp(t2, Y_TO(1)), dp(b2, Y_TO(-1))
    b1, t3 = dp(b1, Y_TO(1)), dp(t3, Y_TO(-1))
    w, _ = lax.optimization_barrier((w, gate))
    p = dp(lax.optimization_barrier(top(w, 1) + u), Y_TO(1))
    q = dp(lax.optimization_barrier(bot(w, 3) + d), Y_TO(-1))
    t3, b1, p, q, w = lax.optimization_barrier((t3, b1, p, q, w))
    return jnp.concatenate([top(w, 0) + t3 + p, bot(w, 0) + b1 + q], axis=0)


def line_z(v, zl, tail=0):
    def piece(k):
        r = lax.dynamic_slice_in_dim(v, (zl ^ k) * 96, 96, 0)
        return jnp.concatenate([r, v[384:]], axis=0) if tail else r

    n = 96 + tail
    both, w = lax.optimization_barrier((jnp.concatenate([piece(3), piece(1)], axis=0), v))
    got = dp(both, Z_XOR(1))
    v = w
    on = dp(piece(2) + got[:n], Z_XOR(2))
    return piece(0) + got[n:] + on


def split_kernel(w, hi, lo):
    hi[...], lo[...] = ksplit(w[...])


def split_rows(w):
    n, m = w.shape
    blk = pl.BlockSpec((n // 8, m), lambda i: (i, 0))
    return pl.pallas_call(
        split_kernel,
        grid=(8,),
        out_shape=(jax.ShapeDtypeStruct((n, m), BF16),) * 2,
        in_specs=[blk],
        out_specs=(blk, blk),
        name="split_rows",
    )(w)


def step(frames, norm_gain, w_in, w_out, head_weight, teacher):
    m = lax.axis_index("mp")
    zh, x, c = m // 8, (m // 2) % 4, m % 2
    d = lax.axis_index("dp")
    y, zl = d // 4, d % 4
    idx = jnp.stack([zh, x, c]).astype(jnp.int32)

    mine, other = gather_blocks(frames.T)

    whi, wlo = split(w_in.T * norm_gain[None, :])
    ohi, olo = split(w_out)
    hhi, hlo = split_rows(head_weight[0])
    gain = lax.dynamic_slice_in_dim(norm_gain, d * 96, 96, 0)[:, None]
    starts = [((x + b) % 4) * 112 + (zh ^ a) * 56 for a in range(2) for b in range(4)]
    target = jnp.concatenate([lax.dynamic_slice_in_dim(teacher[0], s, 56, 0) for s in starts], axis=0)
    other[0], whi, wlo, ohi, olo, target = lax.optimization_barrier(
        (other[0], whi, wlo, ohi, olo, target))

    nt, send, keep, act3, pre = ffn_in(idx, frames, *mine, *other, whi, wlo, ohi, olo)
    mine, other = gather_blocks(reduce_mp(send, keep))
    row3, col3 = join(idx, mine, other)

    codes = jnp.arange(1024, dtype=jnp.int32)
    logits = dot(row3, pair3(hhi, hlo, 0), 1, 0)
    top = jnp.max(logits, axis=1, keepdims=True)
    expo = jnp.exp(logits - top)
    total = jnp.sum(expo, axis=1, keepdims=True)
    lse = top + jnp.log(total)
    onehot = (target[:, None] == codes[None, :]).astype(F32)
    picked = jnp.sum(logits * onehot, axis=1, keepdims=True)
    dlogits = expo / total - onehot
    extra = jnp.full((8, 768), jnp.sum(lse - picked), F32)
    part = dot(left3(dlogits, 1), pair3(hhi, hlo, 1), 1, 1)
    send = lax.dynamic_slice_in_dim(part, (1 - c) * 768, 768, 1)
    keep = lax.dynamic_slice_in_dim(part, c * 768, 768, 1)

    gh = dot(col3, right3(dlogits, 0), 0, 0)
    own = reduce_mp(send, keep)
    mine, other = gather_blocks(jnp.concatenate([own, extra], axis=0))
    gs = ring_y(gh, y, tuple(mine[1:4]))
    grad_head = line_z(gs, zl)
    row3, col3 = join(idx, mine, other)
    loss_mp = sum(v[56:, :384] for v in mine + other)

    go = dot(col3, act3, 0, 0)
    da = dot(row3, pair3(ohi, olo, 1), 1, 1)
    dpre3 = dpre_of(idx, da, pre)
    gi = dot(nt, dpre3, 1, 0)
    grad_outT = line_z(ring_y(go, y, gi), zl)
    r = line_z(ring_y(gi, y, go, loss_mp), zl, 8)
    loss = r[96, 0] / (7168 * 16)
    return (loss, r[:96] * gain, grad_outT.T, grad_head[None])


def solution(mesh):
    placed = (P("dp", "mp"), P(), P(None, "mp"), P("mp", None), P("mp", None, None), P("mp", "dp"))
    return jax.shard_map(
        step,
        mesh=mesh,
        in_specs=placed,
        out_specs=(P(), P("dp", "mp"), P("mp", "dp"), P("mp", "dp", None)),
        check_vma=False,
    )
```
